512 devices in a mesh: head: 8 (over x, core), ctx: 64 (over y, z).
Axes of the slice: x: 4, y: 4, z: 16, core: 2. Of those that a mesh axis runs over, the one named last changes fastest.
Arguments:
- queries: bfloat16 [32768, 4096], P('ctx', 'head'), may hold values from -26.25 to 26.25
- keys: bfloat16 [32768, 1024], P(('ctx', 'head')), may hold values from -7.5 to 7.5
- values: bfloat16 [32768, 1024], P(('ctx', 'head')), may hold values from -5 to 5
- selected: int32 [8, 64, 3], P('head'), may hold values from 0 to 63, as said below
Outputs:
- attended: bfloat16 [32768, 4096], P('ctx', 'head')
The draws below stay inside these ranges and needn't reach their ends.
Inputs may be any that keep to these rules, and one draw needn't show every extreme that they name: `selected`: row b of every key-value head holds b in slot 0; its other 2 slots hold distinct blocks below b, or b again where fewer than 2 blocks lie below b.
All inputs are finite; a program needn't handle non-finite values.
Results may differ from the reference program's by a relative error of at most 0.0041.
Values may be sent and summed in bfloat16 or wider, within the bound.
A program may use at most 64 MiB of HBM per device.

```python
import jax
import jax.numpy as jnp
from jax import lax

HD = 128
QH = 4
BLK = 512
TOPK = 3
KVH = 8
HEADS = 32
TOKENS = 32768
NB = 64


def shared_keys(key):
    base_key = jax.random.fold_in(key, 101)
    drawn = 1.5 * jax.random.truncated_normal(jax.random.fold_in(base_key, 1), -4.0, 4.0, (TOKENS, KVH, HD), jnp.float32)
    return drawn


def draw_keys(key, part):
    mixed = shared_keys(key)
    return mixed.reshape(TOKENS, KVH * HD).astype(jnp.bfloat16)


def draw_queries(key, part):
    drawn = jax.random.truncated_normal(jax.random.fold_in(key, 202), -4.0, 4.0, (TOKENS, HEADS, HD), jnp.float32)
    return drawn.reshape(TOKENS, HEADS * HD).astype(jnp.bfloat16)


def draw_selected(key, part):
    popularity = jax.random.randint(jax.random.fold_in(key, 301), (KVH, 1, NB), 0, 4)
    jitter = jax.random.randint(jax.random.fold_in(key, 302), (KVH, NB, NB), 0, 2 ** 18)
    row_ids = jnp.arange(NB, dtype=jnp.int32)[None, :, None]
    col_ids = jnp.arange(NB, dtype=jnp.int32)[None, None, :]
    earlier = col_ids < row_ids
    ranked = jnp.where(earlier, (jitter + popularity * 2 ** 18) * NB + col_ids, -1 - col_ids)
    picked_score, picked = lax.top_k(ranked, TOPK - 1)
    picked = jnp.where(picked_score >= 0, picked, row_ids)
    own_slot = jnp.broadcast_to(row_ids, (KVH, NB, 1))
    return jnp.concatenate([own_slot, picked.astype(jnp.int32)], axis=2).astype(jnp.int32)


def steps_of(own_key, shape, pieces, low, largest):
    level = 1.0
    for position, blocks in pieces:
        steps = jax.random.uniform(jax.random.fold_in(jax.random.fold_in(own_key, 6), position), (blocks,), jnp.float32, low / len(pieces), largest / len(pieces))
        level = level * jnp.repeat(jnp.exp(steps), shape[position] // blocks).reshape((-1,) + (1,) * (len(shape) - 1 - position))
    return level


def scatter_about(key, dims, scale, bound, split=(), kind=jnp.bfloat16):
    array = scale * jax.random.normal(key, dims, jnp.float32)
    if split:
        array = array * steps_of(key, dims, split, -0.22, 0.18)
    return jnp.clip(array, -bound, bound).astype(kind)


def setup_inputs(seed: int = 0) -> dict:
    seeds = jax.random.split(jax.random.key(seed), 5)
    queries = draw_queries(jax.random.fold_in(seeds[4], 71), 0)
    keys = draw_keys(jax.random.fold_in(seeds[4], 71), 0)
    values = scatter_about(seeds[2], (TOKENS, KVH * HD), 1.0, 5.0, ((0, 512),))
    selected = draw_selected(jax.random.fold_in(seeds[4], 71), 0)
    return {"queries": queries, "keys": keys, "values": values, "selected": selected}


def reference(queries, keys, values, selected):
    blocks_all = TOKENS // BLK
    query_view = queries.reshape(blocks_all, BLK, HEADS, HD)
    key_view = keys.reshape(blocks_all, BLK, KVH, HD)
    value_view = values.reshape(blocks_all, BLK, KVH, HD)
    positions = jnp.arange(BLK, dtype=jnp.int32)
    causal = positions[:, None] >= positions[None, :]
    first_slot = jnp.arange(TOPK, dtype=jnp.int32) == 0
    factor = HD ** -0.5

    def one_pair(pair_index):
        head_id = pair_index // blocks_all
        block_id = pair_index % blocks_all
        group_id = head_id // QH
        chosen = selected[group_id, block_id]
        query_rows = query_view[block_id, :, head_id, :].astype(jnp.float32)
        key_rows = key_view[chosen][:, :, group_id, :].astype(jnp.float32)
        value_rows = value_view[chosen][:, :, group_id, :].astype(jnp.float32)
        scores = jnp.einsum("qd,tkd->qtk", query_rows, key_rows) * factor
        slot_live = first_slot | (chosen != block_id)
        allowed = jnp.where(first_slot[None, :, None], causal[:, None, :], slot_live[None, :, None])
        scores = jnp.where(allowed, scores, -jnp.inf)
        top_score = jnp.max(scores, axis=(1, 2), keepdims=True)
        weights = jnp.exp(scores - top_score)
        weight_sum = jnp.sum(weights, axis=(1, 2))
        rounded = lax.optimization_barrier(weights.astype(jnp.bfloat16)).astype(jnp.float32)
        numerator = jnp.einsum("qtk,tkd->qd", rounded, value_rows)
        return (numerator / weight_sum[:, None]).astype(jnp.bfloat16)

    results = lax.map(one_pair, jnp.arange(HEADS * blocks_all, dtype=jnp.int32))
    results = results.reshape(HEADS, blocks_all, BLK, HD).transpose(1, 2, 0, 3)
    return results.reshape(TOKENS, HEADS * HD)
```

```python
import functools

import jax
import jax.numpy as jnp
from jax import lax
from jax.experimental import pallas as pl
from jax.experimental.pallas import tpu as pltpu
from jax.sharding import PartitionSpec as P

MESH = pl.DeviceIdType.MESH
HD = 128
QH = 4
BLK = 512
KVH = 8
NB = 64
NY = 4
NZ = 16
PIECE = 16
SLICE = BLK // KVH
ROWS = 128
LOG2E = 1.4426950408889634
SCALE = HD ** (-0.5) * LOG2E


def partner(me, t):
    k = NZ - 1 - t // NY
    dy = t % NY
    dz = ((k + 1) // 2) * (2 * (k % 2) - 1)
    return ((me // NZ + dy) % NY) * NZ + (me % NZ + dz + NZ) % NZ


def keeper(head, q):
    return ((head // 2 + q) % NY) * NZ + 2 * q + head % 2


def kept(me):
    y, z = me // NZ, me % NZ
    q = z // 2
    head = ((y + 2 * NY - q) % NY) * 2 + z % 2
    return (q // 4) * 32 + head * 4 + q % 4


def scores(q, k):
    return lax.dot_general(q, k, (((1,), (1,)), ((), ())), preferred_element_type=jnp.float32)


def weighted(p, v):
    ones = jnp.ones_like(v)
    return jnp.dot(p.astype(jnp.bfloat16), jnp.concatenate([v, ones], axis=1), preferred_element_type=jnp.float32)


def kernel(
    queries, keys, values, selected, out,
    q_ref, sel, own, pieces, picked, fetched, top, acc, o_ref,
    q_sem, sel_sem, head_send, head_recv, spread_send, spread_recv, fetch_send, fetch_recv, out_sem,
):
    me = lax.axis_index("ctx")
    head = lax.axis_index("head")
    x, core = head // 2, head % 2

    barrier = pltpu.get_barrier_semaphore()

    def greet(t, carry):
        pl.semaphore_signal(barrier, inc=1, device_id={"ctx": (me + t + 1) % NB}, device_id_type=MESH)
        return carry

    lax.fori_loop(0, NB - 1, greet, 0)
    for j in range(1, KVH):
        pl.semaphore_signal(barrier, inc=1, device_id={"head": (head + j) % KVH}, device_id_type=MESH)

    q_copy = pltpu.make_async_copy(queries, q_ref, q_sem)
    q_copy.start()
    sel_copy = pltpu.make_async_copy(selected, sel, sel_sem)
    sel_copy.start()
    for kv, source in enumerate((keys, values)):
        columns = pl.ds(pl.multiple_of(head * HD, HD), HD)
        pltpu.make_async_copy(source.at[:, columns], own.at[kv, head], head_recv.at[head]).start()
    sel_copy.wait()

    pl.semaphore_wait(barrier, NB - 1 + KVH - 1)

    order = [(dx, dk) for dx in (0, 1, 3, 2) for dk in (0, 1)]
    for dx, dk in order[1:]:
        g = ((x + dx) % 4) * 2 + (core + dk) % 2
        for kv, source in enumerate((keys, values)):
            columns = pl.ds(pl.multiple_of(g * HD, HD), HD)
            pltpu.make_async_remote_copy(
                src_ref=source.at[:, columns], dst_ref=own.at[kv, head], send_sem=head_send,
                recv_sem=head_recv.at[head], device_id={"head": g}, device_id_type=MESH,
            ).start()

    for dx, dk in order:
        g = ((x + (4 - dx)) % 4) * 2 + (core + dk) % 2
        pltpu.make_async_copy(own.at[:, g], own.at[:, g], head_recv.at[g]).wait()
        for q in range(8):
            to = keeper(g, q)
            source = own.at[q // 4, g, pl.ds(PIECE * (q % 4), PIECE)]

            @pl.when(to != me)
            def _():
                pltpu.make_async_remote_copy(
                    src_ref=source, dst_ref=pieces.at[me], send_sem=spread_send,
                    recv_sem=spread_recv, device_id={"ctx": to}, device_id_type=MESH,
                ).start()

            @pl.when(to == me)
            def _():
                pltpu.make_async_copy(source, pieces.at[me], spread_recv).start()

    pltpu.make_async_copy(pieces, pieces, spread_recv).wait()

    def pick(d, carry):
        picked[d, 0] = pieces[sel[0, d, 1]]
        picked[d, 1] = pieces[sel[0, d, 2]]
        return carry

    lax.fori_loop(0, NB, pick, 0)
    mine = kept(me)

    def send(t, carry):
        d = partner(me, t)

        @pl.when(d != me)
        def _():
            pltpu.make_async_remote_copy(
                src_ref=picked.at[d], dst_ref=fetched.at[mine], send_sem=fetch_send,
                recv_sem=fetch_recv, device_id={"ctx": d}, device_id_type=MESH,
            ).start()

        @pl.when(d == me)
        def _():
            pltpu.make_async_copy(picked.at[d], fetched.at[mine], fetch_recv).start()

        return carry

    lax.fori_loop(0, NB, send, 0)

    q_copy.wait()

    def own_block(h, carry):
        columns = pl.ds(pl.multiple_of(h * HD, HD), HD)
        for r in range(BLK // ROWS):
            rows, width = pl.ds(r * ROWS, ROWS), (r + 1) * ROWS
            k = own[0].reshape(BLK, HD)[:width]
            v = own[1].reshape(BLK, HD)[:width]
            s = scores(q_ref[rows, columns], k)
            at = lax.broadcasted_iota(jnp.int32, s.shape, 0) + r * ROWS
            s = jnp.where(lax.broadcasted_iota(jnp.int32, s.shape, 1) <= at, s, -jnp.inf)
            m = jnp.max(s, axis=1, keepdims=True)
            acc[h, rows] = weighted(jnp.exp2((s - m) * SCALE), v)
            top[h, rows] = jnp.broadcast_to(m, (ROWS, HD))
        return carry

    lax.fori_loop(0, QH, own_block, 0)

    pltpu.make_async_copy(fetched, fetched, fetch_recv).wait()
    gone = [jnp.where(sel[0, me, s + 1] != me, 0.0, jnp.inf).astype(jnp.float32) for s in range(2)]

    def others(i, carry):
        h, r = i // (BLK // ROWS), i % (BLK // ROWS)
        columns = pl.ds(pl.multiple_of(h * HD, HD), HD)
        rows = pl.ds(pl.multiple_of(r * ROWS, ROWS), ROWS)
        q = q_ref[rows, columns]
        m0 = top[h, rows][:, :1]
        m = m0
        parts = []
        for s in range(2):
            part = scores(q, fetched[:32, s].reshape(BLK, HD))
            m = jnp.maximum(m, jnp.max(part, axis=1, keepdims=True) - gone[s])
            parts.append(part)
        total = acc[h, rows] * jnp.exp2((m0 - m) * SCALE)
        for s in range(2):
            p = jnp.exp2((parts[s] - (m + gone[s])) * SCALE)
            total += weighted(p, fetched[32:, s].reshape(BLK, HD))
        o_ref[rows, columns] = (total[:, :HD] / total[:, HD:]).astype(o_ref.dtype)
        return carry

    lax.fori_loop(0, QH * BLK // ROWS, others, 0)
    out_copy = pltpu.make_async_copy(o_ref, out, out_sem)
    out_copy.start()

    most = pl.ds(0, KVH - 1)
    pltpu.make_async_copy(own.at[:, most], own.at[:, most], head_send).wait()
    most = pl.ds(0, NB - 1)
    pltpu.make_async_copy(pieces.at[most], pieces.at[most], spread_send).wait()
    pltpu.make_async_copy(picked.at[most], picked.at[most], fetch_send).wait()
    out_copy.wait()


def on_device(queries, keys, values, selected):
    dma = pltpu.SemaphoreType.DMA
    hbm = pl.BlockSpec(memory_space=pl.ANY)
    return pl.pallas_call(
        kernel,
        out_shape=jax.ShapeDtypeStruct((BLK, QH * HD), jnp.bfloat16),
        in_specs=[hbm, hbm, hbm, hbm],
        out_specs=hbm,
        scratch_shapes=[
            pltpu.VMEM((BLK, QH * HD), jnp.bfloat16),
            pltpu.SMEM((1, NB, 3), jnp.int32),
            pltpu.VMEM((2, KVH, SLICE, HD), jnp.bfloat16),
            pltpu.VMEM((NB, PIECE, HD), jnp.bfloat16),
            pltpu.VMEM((NB, 2, PIECE, HD), jnp.bfloat16),
            pltpu.VMEM((NB, 2, PIECE, HD), jnp.bfloat16),
            pltpu.VMEM((QH, BLK, HD), jnp.float32),
            pltpu.VMEM((QH, BLK, 2 * HD), jnp.float32),
            pltpu.VMEM((BLK, QH * HD), jnp.bfloat16),
            dma, dma, dma, dma((KVH,)), dma, dma, dma, dma, dma,
        ],
        compiler_params=pltpu.CompilerParams(collective_id=0, has_side_effects=True),
    )(queries, keys, values, selected)


def solution(mesh):
    return jax.shard_map(
        on_device,
        mesh=mesh,
        in_specs=(
            P("ctx", "head"),
            P(("ctx", "head"), None),
            P(("ctx", "head"), None),
            P("head", None, None),
        ),
        out_specs=P("ctx", "head"),
        check_vma=False,
    )
```

```python
import functools

import jax
import jax.numpy as jnp
from jax import lax
from jax.experimental import pallas as pl
from jax.experimental.pallas import tpu as pltpu
from jax.sharding import PartitionSpec as P

MESH = pl.DeviceIdType.MESH
HD = 128
QH = 4
BLK = 512
KVH = 8
NB = 64
NY = 4
NZ = 16
GROUPS = 4
PIECE = 16
SLICE = BLK // KVH
ROWS = 128
LOG2E = 1.4426950408889634
SCALE = HD ** (-0.5) * LOG2E


STEPS = [8, 9, 7, 10, 6, 11, 5, 12, 4, 13, 3, 14, 2, 15, 1, 0]
AHEAD = 8


def kept(me):
    w = (me // NZ + NY - (me % NZ) // 4) % NY
    return w // 2, w % 2


def part(q_t, k, v, mask, before):
    s = jnp.dot(k, q_t, preferred_element_type=jnp.float32)
    if mask is not None:
        s = mask(s)
    m = jnp.max(s, axis=0, keepdims=True)
    if before is not None:
        m = jnp.maximum(m, before[0])
    p = jnp.exp2((s - m) * SCALE).astype(jnp.bfloat16)
    v_t = jnp.concatenate([v.T, jnp.ones((PIECE, v.shape[0]), v.dtype)], axis=0)
    total = jnp.dot(v_t, p, preferred_element_type=jnp.float32)
    if before is not None:
        total += before[1] * jnp.exp2((before[0] - m) * SCALE)
    return m, total


def kernel(
    queries, keys, values, selected, out,
    q_ref, q_t, sel, own, pieces, picked, fetched, top, acc,
    q_sem, sel_sem, head_send, head_recv, spread_send, spread_recv, fetch_send, fetch_recv,
):
    me = lax.axis_index("ctx")
    head = lax.axis_index("head")
    x, core = head // 2, head % 2

    barrier = pltpu.get_barrier_semaphore()

    y, z = me // NZ, me % NZ
    rows_y = [((y + j) % NY) * NZ for j in range(NY)]
    others = [(n, rows_y[j] + z_to) for n, z_to in enumerate((z + dz) % NZ for dz in STEPS) for j in (2, 1, 3, 0)][:-1]
    for _, to in others:
        pl.semaphore_signal(barrier, inc=1, device_id={"ctx": to}, device_id_type=MESH)
    for j in range(1, KVH):
        pl.semaphore_signal(barrier, inc=1, device_id={"head": (head + j) % KVH}, device_id_type=MESH)

    q_copy = pltpu.make_async_copy(queries, q_ref, q_sem)
    q_copy.start()
    sel_copy = pltpu.make_async_copy(selected, sel, sel_sem)
    sel_copy.start()
    for kv, source in enumerate((keys, values)):
        columns = pl.ds(pl.multiple_of(head * HD, HD), HD)
        pltpu.make_async_copy(source.at[:, columns], own.at[kv, head], head_recv.at[head]).start()
    sel_copy.wait()

    pl.semaphore_wait(barrier, NB - 1 + KVH - 1)

    order = [(dx, dk) for dx in (0, 1, 3, 2) for dk in (0, 1)]
    for dx, dk in order[1:]:
        g = ((x + dx) % 4) * 2 + (core + dk) % 2
        for kv, source in enumerate((keys, values)):
            columns = pl.ds(pl.multiple_of(g * HD, HD), HD)
            pltpu.make_async_remote_copy(
                src_ref=source.at[:, columns], dst_ref=own.at[kv, head], send_sem=head_send,
                recv_sem=head_recv.at[head], device_id={"head": g}, device_id_type=MESH,
            ).start()

    for dx, dk in order:
        g = ((x + (4 - dx)) % 4) * 2 + (core + dk) % 2
        pltpu.make_async_copy(own.at[:, g], own.at[:, g], head_recv.at[g]).wait()
        for off in (2, 1, 3, 0):
            j = (z // 4 + off) % 4
            for kv in range(2):
                to = ((2 * kv + g // 4 + j) % NY) * NZ + 4 * j + g % 4
                source = own.at[kv, g, pl.ds(pl.multiple_of(PIECE * j, PIECE), PIECE)]

                def remote(source=source, to=to):
                    pltpu.make_async_remote_copy(
                        src_ref=source, dst_ref=pieces.at[me], send_sem=spread_send,
                        recv_sem=spread_recv, device_id={"ctx": to}, device_id_type=MESH,
                    ).start()

                if off:
                    remote()
                else:
                    pl.when(to != me)(remote)

                    @pl.when(to == me)
                    def _():
                        pltpu.make_async_copy(source, pieces.at[me], spread_recv).start()

    pltpu.make_async_copy(pieces, pieces, spread_recv).wait()

    kv, half = kept(me)

    def pick(d):
        picked[d, 0] = pieces[sel[1, 0, d]]
        picked[d, 1] = pieces[sel[2, 0, d]]

    per_group = NZ // GROUPS
    for _, d in others[:AHEAD]:
        pick(d)
    for t, (n, d) in enumerate(others):
        pltpu.make_async_remote_copy(
            src_ref=picked.at[d], dst_ref=fetched.at[n, kv, half], send_sem=fetch_send,
            recv_sem=fetch_recv.at[n // per_group], device_id={"ctx": d}, device_id_type=MESH,
        ).start()
        if t + AHEAD < NB - 1:
            pick(others[t + AHEAD][1])
    last = NZ - 1
    pick(me)

    q_copy.wait()
    pltpu.make_async_copy(picked.at[me], fetched.at[last, kv, half], fetch_recv.at[GROUPS - 1]).start()
    for h in range(QH):
        q_t[:, h * BLK : (h + 1) * BLK] = q_ref[:, h * HD : (h + 1) * HD].T
    half_block = BLK // 2
    before = None
    for c in range(2):
        low = c * half_block

        def causal(s):
            key = lax.broadcasted_iota(jnp.int32, s.shape, 0) + low
            return jnp.where(key <= lax.broadcasted_iota(jnp.int32, s.shape, 1) % BLK, s, -jnp.inf)

        k = own[0].reshape(BLK, HD)[low : low + half_block]
        v = own[1].reshape(BLK, HD)[low : low + half_block]
        before = part(q_t[...], k, v, causal, before)
        top[...], acc[...] = before
        before = top[...], acc[...]

    gone = [jnp.where(sel[s + 1, 0, me] != me, 0.0, -jnp.inf).astype(jnp.float32) for s in range(2)]
    shape = (NB // NY // GROUPS * 4, PIECE, 1)
    slot = lax.broadcasted_iota(jnp.int32, shape, 0) % 2
    bias = jnp.where(slot == 0, gone[0], gone[1]).reshape(shape[0] * PIECE, 1)
    for g in range(GROUPS):
        planes = slice(g * (NZ // GROUPS), (g + 1) * (NZ // GROUPS))
        pltpu.make_async_copy(fetched.at[planes], fetched.at[planes], fetch_recv.at[g]).wait()
        k = fetched[planes, 0].reshape(-1, HD)
        v = fetched[planes, 1].reshape(-1, HD)
        before = part(q_t[...], k, v, lambda s: s + bias, (top[...], acc[...]))
        if g < GROUPS - 1:
            top[...], acc[...] = before
    total = before[1]
    for h in range(QH):
        t = total[:, h * BLK : (h + 1) * BLK]
        columns = slice(h * HD, (h + 1) * HD)
        out[:, columns] = (t[:HD] / t[HD : HD + 1]).astype(out.dtype).T

    most = pl.ds(0, KVH - 1)
    pltpu.make_async_copy(own.at[:, most], own.at[:, most], head_send).wait()
    most = pl.ds(0, NB - 1)
    pltpu.make_async_copy(pieces.at[most], pieces.at[most], spread_send).wait()
    pltpu.make_async_copy(picked.at[most], picked.at[most], fetch_send).wait()


def on_device(queries, keys, values, selected):
    dma = pltpu.SemaphoreType.DMA
    hbm = pl.BlockSpec(memory_space=pl.ANY)
    return pl.pallas_call(
        kernel,
        out_shape=pltpu.VMEM((BLK, QH * HD), jnp.bfloat16),
        in_specs=[hbm, hbm, hbm, hbm],
        out_specs=pl.BlockSpec(memory_space=pltpu.VMEM),
        scratch_shapes=[
            pltpu.VMEM((BLK, QH * HD), jnp.bfloat16),
            pltpu.VMEM((HD, QH * BLK), jnp.bfloat16),
            pltpu.SMEM((3, 1, NB), jnp.int32),
            pltpu.VMEM((2, KVH, SLICE, HD), jnp.bfloat16),
            pltpu.VMEM((NB, PIECE, HD), jnp.bfloat16),
            pltpu.VMEM((NB, 2, PIECE, HD), jnp.bfloat16),
            pltpu.VMEM((NZ, 2, 2, 2, PIECE, HD), jnp.bfloat16),
            pltpu.VMEM((1, QH * BLK), jnp.float32),
            pltpu.VMEM((HD + PIECE, QH * BLK), jnp.float32),
            dma, dma, dma, dma((KVH,)), dma, dma, dma, dma((GROUPS,)),
        ],
        compiler_params=pltpu.CompilerParams(collective_id=0, has_side_effects=True),
    )(queries, keys, values, selected.transpose(2, 0, 1))


def solution(mesh):
    return jax.shard_map(
        on_device,
        mesh=mesh,
        in_specs=(
            P("ctx", "head"),
            P(("ctx", "head"), None),
            P(("ctx", "head"), None),
            P("head", None, None),
        ),
        out_specs=P("ctx", "head"),
        check_vma=False,
    )
```

```python
import functools

import jax
import jax.numpy as jnp
from jax import lax
from jax.experimental import pallas as pl
from jax.experimental.pallas import tpu as pltpu
from jax.sharding import PartitionSpec as P

MESH = pl.DeviceIdType.MESH
HD = 128
QH = 4
BLK = 512
KVH = 8
NB = 64
NY = 4
NZ = 16
GROUPS = 4
PIECE = 16
SLICE = BLK // KVH
ROWS = 128
LOG2E = 1.4426950408889634
SCALE = HD ** (-0.5) * LOG2E


STEPS = [8, 9, 7, 10, 6, 11, 5, 12, 4, 13, 3, 14, 2, 15, 1, 0]
AHEAD = 8


def kept(me):
    w = (me // NZ + NY - (me % NZ) // 4) % NY
    return w // 2, w % 2


def part(q_t, k, v, mask, before):
    s = jnp.dot(k, q_t, preferred_element_type=jnp.float32)
    if mask is not None:
        s = mask(s)
    m = jnp.max(s, axis=0, keepdims=True)
    if before is not None:
        m = jnp.maximum(m, before[0])
    p = jnp.exp2((s - m) * SCALE).astype(jnp.bfloat16)
    v_t = jnp.concatenate([v.T, jnp.ones((PIECE, v.shape[0]), v.dtype)], axis=0)
    total = jnp.dot(v_t, p, preferred_element_type=jnp.float32)
    if before is not None:
        total += before[1] * jnp.exp2((before[0] - m) * SCALE)
    return m, total


def kernel(
    queries, keys, values, selected, out,
    q_ref, q_t, sel, own, pieces, picked, fetched, top, acc,
    q_sem, sel_sem, head_send, head_recv, spread_send, spread_recv, fetch_send, fetch_recv,
):
    me = lax.axis_index("ctx")
    head = lax.axis_index("head")
    x, core = head // 2, head % 2

    barrier = pltpu.get_barrier_semaphore()

    y, z = me // NZ, me % NZ
    rows_y = [((y + j) % NY) * NZ for j in range(NY)]
    others = [(n, rows_y[j] + z_to) for n, z_to in enumerate((z + dz + core * (NZ - 2 * dz) + NZ) % NZ for dz in STEPS) for j in (2, 1, 3, 0)][:-1]
    for _, to in others:
        pl.semaphore_signal(barrier, inc=1, device_id={"ctx": to}, device_id_type=MESH)
    for j in range(1, KVH):
        pl.semaphore_signal(barrier, inc=1, device_id={"head": (head + j) % KVH}, device_id_type=MESH)

    q_copy = pltpu.make_async_copy(queries, q_ref, q_sem)
    q_copy.start()
    sel_copy = pltpu.make_async_copy(selected, sel, sel_sem)
    sel_copy.start()
    for kv, source in enumerate((keys, values)):
        columns = pl.ds(pl.multiple_of(head * HD, HD), HD)
        pltpu.make_async_copy(source.at[:, columns], own.at[kv, head], head_recv.at[head]).start()
    sel_copy.wait()

    pl.semaphore_wait(barrier, NB - 1 + KVH - 1)

    order = [(dx, dk) for dx in (0, 1, 3, 2) for dk in (0, 1)]
    for dx, dk in order[1:]:
        g = ((x + dx) % 4) * 2 + (core + dk) % 2
        for kv, source in enumerate((keys, values)):
            columns = pl.ds(pl.multiple_of(g * HD, HD), HD)
            pltpu.make_async_remote_copy(
                src_ref=source.at[:, columns], dst_ref=own.at[kv, head], send_sem=head_send,
                recv_sem=head_recv.at[head], device_id={"head": g}, device_id_type=MESH,
            ).start()

    for dx, dk in order:
        g = ((x + (4 - dx)) % 4) * 2 + (core + dk) % 2
        pltpu.make_async_copy(own.at[:, g], own.at[:, g], head_recv.at[g]).wait()
        for off in (2, 1, 3, 0):
            j = (z // 4 + off) % 4
            for kv in range(2):
                to = ((2 * kv + g // 4 + j) % NY) * NZ + 4 * j + g % 4
                source = own.at[kv, g, pl.ds(pl.multiple_of(PIECE * j, PIECE), PIECE)]

                def remote(source=source, to=to):
                    pltpu.make_async_remote_copy(
                        src_ref=source, dst_ref=pieces.at[me], send_sem=spread_send,
                        recv_sem=spread_recv, device_id={"ctx": to}, device_id_type=MESH,
                    ).start()

                if off:
                    remote()
                else:
                    pl.when(to != me)(remote)

                    @pl.when(to == me)
                    def _():
                        pltpu.make_async_copy(source, pieces.at[me], spread_recv).start()

    q_copy.wait()
    for h in range(QH):
        q_t[:, h * BLK : (h + 1) * BLK] = q_ref[:, h * HD : (h + 1) * HD].T
    half_block = BLK // 2
    before = None
    for c in range(2):
        low = c * half_block

        def causal(s):
            key = lax.broadcasted_iota(jnp.int32, s.shape, 0) + low
            return jnp.where(key <= lax.broadcasted_iota(jnp.int32, s.shape, 1) % BLK, s, -jnp.inf)

        k = own[0].reshape(BLK, HD)[low : low + half_block]
        v = own[1].reshape(BLK, HD)[low : low + half_block]
        before = part(q_t[...], k, v, causal, before)
        top[...], acc[...] = before
        before = top[...], acc[...]

    pltpu.make_async_copy(pieces, pieces, spread_recv).wait()

    kv, half = kept(me)

    def pick(d):
        picked[d, 0] = pieces[sel[1, 0, d]]
        picked[d, 1] = pieces[sel[2, 0, d]]

    per_group = NZ // GROUPS
    pick(me)
    for _, d in others[:AHEAD]:
        pick(d)
    for t, (n, d) in enumerate(others):
        pltpu.make_async_remote_copy(
            src_ref=picked.at[d], dst_ref=fetched.at[n, kv, half], send_sem=fetch_send,
            recv_sem=fetch_recv.at[n // per_group], device_id={"ctx": d}, device_id_type=MESH,
        ).start()
        if t + AHEAD < NB - 1:
            pick(others[t + AHEAD][1])
    last = NZ - 1

    pltpu.make_async_copy(picked.at[me], fetched.at[last, kv, half], fetch_recv.at[GROUPS - 1]).start()
    gone = [jnp.where(sel[s + 1, 0, me] != me, 0.0, -jnp.inf).astype(jnp.float32) for s in range(2)]
    shape = (NB // NY // GROUPS * 4, PIECE, 1)
    slot = lax.broadcasted_iota(jnp.int32, shape, 0) % 2
    bias = jnp.where(slot == 0, gone[0], gone[1]).reshape(shape[0] * PIECE, 1)
    for g in range(GROUPS):
        planes = slice(g * (NZ // GROUPS), (g + 1) * (NZ // GROUPS))
        pltpu.make_async_copy(fetched.at[planes], fetched.at[planes], fetch_recv.at[g]).wait()
        k = fetched[planes, 0].reshape(-1, HD)
        v = fetched[planes, 1].reshape(-1, HD)
        before = part(q_t[...], k, v, lambda s: s + bias, (top[...], acc[...]))
        if g < GROUPS - 1:
            top[...], acc[...] = before
    total = before[1]
    for h in range(QH):
        t = total[:, h * BLK : (h + 1) * BLK]
        columns = slice(h * HD, (h + 1) * HD)
        out[:, columns] = (t[:HD] / t[HD : HD + 1]).astype(out.dtype).T

    most = pl.ds(0, KVH - 1)
    pltpu.make_async_copy(own.at[:, most], own.at[:, most], head_send).wait()
    most = pl.ds(0, NB - 1)
    pltpu.make_async_copy(pieces.at[most], pieces.at[most], spread_send).wait()
    pltpu.make_async_copy(picked.at[most], picked.at[most], fetch_send).wait()


def on_device(queries, keys, values, selected):
    dma = pltpu.SemaphoreType.DMA
    hbm = pl.BlockSpec(memory_space=pl.ANY)
    return pl.pallas_call(
        kernel,
        out_shape=pltpu.VMEM((BLK, QH * HD), jnp.bfloat16),
        in_specs=[hbm, hbm, hbm, hbm],
        out_specs=pl.BlockSpec(memory_space=pltpu.VMEM),
        scratch_shapes=[
            pltpu.VMEM((BLK, QH * HD), jnp.bfloat16),
            pltpu.VMEM((HD, QH * BLK), jnp.bfloat16),
            pltpu.SMEM((3, 1, NB), jnp.int32),
            pltpu.VMEM((2, KVH, SLICE, HD), jnp.bfloat16),
            pltpu.VMEM((NB, PIECE, HD), jnp.bfloat16),
            pltpu.VMEM((NB, 2, PIECE, HD), jnp.bfloat16),
            pltpu.VMEM((NZ, 2, 2, 2, PIECE, HD), jnp.bfloat16),
            pltpu.VMEM((1, QH * BLK), jnp.float32),
            pltpu.VMEM((HD + PIECE, QH * BLK), jnp.float32),
            dma, dma, dma, dma((KVH,)), dma, dma, dma, dma((GROUPS,)),
        ],
        compiler_params=pltpu.CompilerParams(collective_id=0, has_side_effects=True),
    )(queries, keys, values, selected.transpose(2, 0, 1))


def solution(mesh):
    return jax.shard_map(
        on_device,
        mesh=mesh,
        in_specs=(
            P("ctx", "head"),
            P(("ctx", "head"), None),
            P(("ctx", "head"), None),
            P("head", None, None),
        ),
        out_specs=P("ctx", "head"),
        check_vma=False,
    )
```

```python
import functools

import jax
import jax.numpy as jnp
from jax import lax
from jax.experimental import pallas as pl
from jax.experimental.pallas import tpu as pltpu
from jax.sharding import PartitionSpec as P

MESH = pl.DeviceIdType.MESH
HD = 128
QH = 4
BLK = 512
KVH = 8
NB = 64
NY = 4
NZ = 16
GROUPS = 4
PIECE = 16
SLICE = BLK // KVH
ROWS = 128
LOG2E = 1.4426950408889634
SCALE = HD ** (-0.5) * LOG2E


STEPS = [8, 9, 7, 10, 6, 11, 5, 12, 4, 13, 3, 14, 2, 15, 1, 0]
AHEAD = 8


def kept(me):
    w = (me // NZ + NY - (me % NZ) // 4) % NY
    return w // 2, w % 2


def part(q_t, k, v, mask, before):
    s = jnp.dot(k, q_t, preferred_element_type=jnp.float32)
    if mask is not None:
        s = mask(s)
    m = jnp.max(s, axis=0, keepdims=True)
    if before is not None:
        m = jnp.maximum(m, before[0])
    p = jnp.exp2((s - m) * SCALE).astype(jnp.bfloat16)
    v_t = jnp.concatenate([v.T, jnp.ones((PIECE, v.shape[0]), v.dtype)], axis=0)
    total = jnp.dot(v_t, p, preferred_element_type=jnp.float32)
    if before is not None:
        total += before[1] * jnp.exp2((before[0] - m) * SCALE)
    return m, total


def kernel(
    queries, keys, values, selected, out,
    q_ref, q_t, sel, own, pieces, picked, fetched, top, acc,
    q_sem, sel_sem, head_send, head_recv, spread_send, spread_recv, fetch_send, fetch_recv,
):
    me = lax.axis_index("ctx")
    head = lax.axis_index("head")
    x, core = head // 2, head % 2

    barrier = pltpu.get_barrier_semaphore()

    y, z = me // NZ, me % NZ
    rows_y = [((y + j) % NY) * NZ for j in range(NY)]
    others = [(n, rows_y[j] + z_to) for n, z_to in enumerate((z + dz + core * (NZ - 2 * dz) + NZ) % NZ for dz in STEPS) for j in (2, 1, 3, 0)][:-1]
    for _, to in others:
        pl.semaphore_signal(barrier, inc=1, device_id={"ctx": to}, device_id_type=MESH)
    for j in range(1, KVH):
        pl.semaphore_signal(barrier, inc=1, device_id={"head": (head + j) % KVH}, device_id_type=MESH)

    q_copy = pltpu.make_async_copy(queries, q_ref, q_sem)
    q_copy.start()
    sel_copy = pltpu.make_async_copy(selected, sel, sel_sem)
    sel_copy.start()
    for kv, source in enumerate((keys, values)):
        columns = pl.ds(pl.multiple_of(head * HD, HD), HD)
        pltpu.make_async_copy(source.at[:, columns], own.at[kv, head], head_recv.at[head]).start()
    sel_copy.wait()

    pl.semaphore_wait(barrier, NB - 1 + KVH - 1)

    order = [(0, 0), (0, 1), (1, 0), (3, 0), (1, 1), (3, 1), (2, 0), (2, 1)]
    for dx, dk in order[1:]:
        g = ((x + dx) % 4) * 2 + (core + dk) % 2
        for kv, source in enumerate((keys, values)):
            columns = pl.ds(pl.multiple_of(g * HD, HD), HD)
            pltpu.make_async_remote_copy(
                src_ref=source.at[:, columns], dst_ref=own.at[kv, head], send_sem=head_send,
                recv_sem=head_recv.at[head], device_id={"head": g}, device_id_type=MESH,
            ).start()

    for dx, dk in order:
        g = ((x + (4 - dx)) % 4) * 2 + (core + dk) % 2
        pltpu.make_async_copy(own.at[:, g], own.at[:, g], head_recv.at[g]).wait()
        for off in (2, 1, 3, 0):
            j = (z // 4 + off) % 4
            for kv in range(2):
                to = ((2 * kv + g // 4 + j) % NY) * NZ + 4 * j + g % 4
                source = own.at[kv, g, pl.ds(pl.multiple_of(PIECE * j, PIECE), PIECE)]

                def remote(source=source, to=to):
                    pltpu.make_async_remote_copy(
                        src_ref=source, dst_ref=pieces.at[me], send_sem=spread_send,
                        recv_sem=spread_recv, device_id={"ctx": to}, device_id_type=MESH,
                    ).start()

                if off:
                    remote()
                else:
                    pl.when(to != me)(remote)

                    @pl.when(to == me)
                    def _():
                        pltpu.make_async_copy(source, pieces.at[me], spread_recv).start()

    q_copy.wait()
    for h in range(QH):
        q_t[:, h * BLK : (h + 1) * BLK] = q_ref[:, h * HD : (h + 1) * HD].T
    half_block = BLK // 2
    before = None
    for c in range(2):
        low = c * half_block

        def causal(s):
            key = lax.broadcasted_iota(jnp.int32, s.shape, 0) + low
            return jnp.where(key <= lax.broadcasted_iota(jnp.int32, s.shape, 1) % BLK, s, -jnp.inf)

        k = own[0].reshape(BLK, HD)[low : low + half_block]
        v = own[1].reshape(BLK, HD)[low : low + half_block]
        before = part(q_t[...], k, v, causal, before)
        top[...], acc[...] = before
        before = top[...], acc[...]

    pltpu.make_async_copy(pieces, pieces, spread_recv).wait()

    kv, half = kept(me)

    def pick(d):
        picked[d, 0] = pieces[sel[1, 0, d]]
        picked[d, 1] = pieces[sel[2, 0, d]]

    per_group = NZ // GROUPS
    pick(me)
    for _, d in others[:AHEAD]:
        pick(d)
    for t, (n, d) in enumerate(others):
        pltpu.make_async_remote_copy(
            src_ref=picked.at[d], dst_ref=fetched.at[n, kv, half], send_sem=fetch_send,
            recv_sem=fetch_recv.at[n // per_group], device_id={"ctx": d}, device_id_type=MESH,
        ).start()
        if t + AHEAD < NB - 1:
            pick(others[t + AHEAD][1])
    last = NZ - 1

    pltpu.make_async_copy(picked.at[me], fetched.at[last, kv, half], fetch_recv.at[GROUPS - 1]).start()
    gone = [jnp.where(sel[s + 1, 0, me] != me, 0.0, -jnp.inf).astype(jnp.float32) for s in range(2)]
    shape = (NB // NY // GROUPS * 4, PIECE, 1)
    slot = lax.broadcasted_iota(jnp.int32, shape, 0) % 2
    bias = jnp.where(slot == 0, gone[0], gone[1]).reshape(shape[0] * PIECE, 1)
    for g in range(GROUPS):
        planes = slice(g * (NZ // GROUPS), (g + 1) * (NZ // GROUPS))
        pltpu.make_async_copy(fetched.at[planes], fetched.at[planes], fetch_recv.at[g]).wait()
        k = fetched[planes, 0].reshape(-1, HD)
        v = fetched[planes, 1].reshape(-1, HD)
        before = part(q_t[...], k, v, lambda s: s + bias, (top[...], acc[...]))
        if g < GROUPS - 1:
            top[...], acc[...] = before
    total = before[1]
    for h in range(QH):
        t = total[:, h * BLK : (h + 1) * BLK]
        columns = slice(h * HD, (h + 1) * HD)
        out[:, columns] = (t[:HD] / t[HD : HD + 1]).astype(out.dtype).T

    most = pl.ds(0, KVH - 1)
    pltpu.make_async_copy(own.at[:, most], own.at[:, most], head_send).wait()
    most = pl.ds(0, NB - 1)
    pltpu.make_async_copy(pieces.at[most], pieces.at[most], spread_send).wait()
    pltpu.make_async_copy(picked.at[most], picked.at[most], fetch_send).wait()


def on_device(queries, keys, values, selected):
    dma = pltpu.SemaphoreType.DMA
    hbm = pl.BlockSpec(memory_space=pl.ANY)
    return pl.pallas_call(
        kernel,
        out_shape=pltpu.VMEM((BLK, QH * HD), jnp.bfloat16),
        in_specs=[hbm, hbm, hbm, hbm],
        out_specs=pl.BlockSpec(memory_space=pltpu.VMEM),
        scratch_shapes=[
            pltpu.VMEM((BLK, QH * HD), jnp.bfloat16),
            pltpu.VMEM((HD, QH * BLK), jnp.bfloat16),
            pltpu.SMEM((3, 1, NB), jnp.int32),
            pltpu.VMEM((2, KVH, SLICE, HD), jnp.bfloat16),
            pltpu.VMEM((NB, PIECE, HD), jnp.bfloat16),
            pltpu.VMEM((NB, 2, PIECE, HD), jnp.bfloat16),
            pltpu.VMEM((NZ, 2, 2, 2, PIECE, HD), jnp.bfloat16),
            pltpu.VMEM((1, QH * BLK), jnp.float32),
            pltpu.VMEM((HD + PIECE, QH * BLK), jnp.float32),
            dma, dma, dma, dma((KVH,)), dma, dma, dma, dma((GROUPS,)),
        ],
        compiler_params=pltpu.CompilerParams(collective_id=0, has_side_effects=True),
    )(queries, keys, values, selected.transpose(2, 0, 1))


def solution(mesh):
    return jax.shard_map(
        on_device,
        mesh=mesh,
        in_specs=(
            P("ctx", "head"),
            P(("ctx", "head"), None),
            P(("ctx", "head"), None),
            P("head", None, None),
        ),
        out_specs=P("ctx", "head"),
        check_vma=False,
    )
```

```python
import functools

import jax
import jax.numpy as jnp
from jax import lax
from jax.experimental import pallas as pl
from jax.experimental.pallas import tpu as pltpu
from jax.sharding import PartitionSpec as P

MESH = pl.DeviceIdType.MESH
HD = 128
QH = 4
BLK = 512
KVH = 8
NB = 64
NY = 4
NZ = 16
GROUPS = 4
PIECE = 16
SLICE = BLK // KVH
ROWS = 128
LOG2E = 1.4426950408889634
SCALE = HD ** (-0.5) * LOG2E


STEPS = [8, 9, 7, 10, 6, 11, 5, 12, 4, 13, 3, 14, 2, 15, 1, 0]
AHEAD = 8


def kept(me):
    w = (me // NZ + NY - (me % NZ) // 4) % NY
    return w // 2, w % 2


def part(q_t, k, v, mask, before):
    s = jnp.dot(k, q_t, preferred_element_type=jnp.float32)
    if mask is not None:
        s = mask(s)
    m = jnp.max(s, axis=0, keepdims=True)
    if before is not None:
        m = jnp.maximum(m, before[0])
    p = jnp.exp2((s - m) * SCALE).astype(jnp.bfloat16)
    v_t = jnp.concatenate([v.T, jnp.ones((PIECE, v.shape[0]), v.dtype)], axis=0)
    total = jnp.dot(v_t, p, preferred_element_type=jnp.float32)
    if before is not None:
        total += before[1] * jnp.exp2((before[0] - m) * SCALE)
    return m, total


def kernel(
    queries, keys, values, selected, out,
    q_ref, q_t, sel, own, pieces, picked, fetched, top, acc,
    q_sem, sel_sem, head_send, head_recv, spread_send, spread_recv, fetch_send, fetch_recv,
):
    me = lax.axis_index("ctx")
    head = lax.axis_index("head")
    x, core = head // 2, head % 2

    barrier = pltpu.get_barrier_semaphore()

    y, z = me // NZ, me % NZ
    rows_y = [((y + j) % NY) * NZ for j in range(NY)]
    others = [(n, rows_y[j] + z_to) for n, z_to in enumerate((z + dz + core * (NZ - 2 * dz) + NZ) % NZ for dz in STEPS) for j in (2, 1, 3, 0)][:-1]
    for _, to in others:
        pl.semaphore_signal(barrier, inc=1, device_id={"ctx": to}, device_id_type=MESH)
    for j in range(1, KVH):
        pl.semaphore_signal(barrier, inc=1, device_id={"head": (head + j) % KVH}, device_id_type=MESH)

    q_copy = pltpu.make_async_copy(queries, q_ref, q_sem)
    q_copy.start()
    sel_copy = pltpu.make_async_copy(selected, sel, sel_sem)
    sel_copy.start()
    for kv, source in enumerate((keys, values)):
        columns = pl.ds(pl.multiple_of(head * HD, HD), HD)
        pltpu.make_async_copy(source.at[:, columns], own.at[kv, head], head_recv.at[head]).start()
    sel_copy.wait()

    pl.semaphore_wait(barrier, NB - 1 + KVH - 1)

    order = [(dx, dk) for dx in (0, 1, 3, 2) for dk in (0, 1)]
    for dx, dk in order[1:]:
        g = ((x + dx) % 4) * 2 + (core + dk) % 2
        for kv, source in enumerate((keys, values)):
            columns = pl.ds(pl.multiple_of(g * HD, HD), HD)
            pltpu.make_async_remote_copy(
                src_ref=source.at[:, columns], dst_ref=own.at[kv, head], send_sem=head_send,
                recv_sem=head_recv.at[head], device_id={"head": g}, device_id_type=MESH,
            ).start()

    for dx, dk in order:
        g = ((x + (4 - dx)) % 4) * 2 + (core + dk) % 2
        pltpu.make_async_copy(own.at[:, g], own.at[:, g], head_recv.at[g]).wait()
        for off in (2, 1, 3, 0):
            j = (z // 4 + off) % 4
            for kv in range(2):
                to = ((2 * kv + g // 4 + j) % NY) * NZ + 4 * j + g % 4
                source = own.at[kv, g, pl.ds(pl.multiple_of(PIECE * j, PIECE), PIECE)]

                def remote(source=source, to=to):
                    pltpu.make_async_remote_copy(
                        src_ref=source, dst_ref=pieces.at[me], send_sem=spread_send,
                        recv_sem=spread_recv, device_id={"ctx": to}, device_id_type=MESH,
                    ).start()

                if off:
                    remote()
                else:
                    pl.when(to != me)(remote)

                    @pl.when(to == me)
                    def _():
                        pltpu.make_async_copy(source, pieces.at[me], spread_recv).start()

    q_copy.wait()
    for h in range(QH):
        q_t[:, h * BLK : (h + 1) * BLK] = q_ref[:, h * HD : (h + 1) * HD].T
    half_block = BLK // 2
    before = None
    for c in range(2):
        low = c * half_block

        def causal(s):
            key = lax.broadcasted_iota(jnp.int32, s.shape, 0) + low
            return jnp.where(key <= lax.broadcasted_iota(jnp.int32, s.shape, 1) % BLK, s, -jnp.inf)

        k = own[0].reshape(BLK, HD)[low : low + half_block]
        v = own[1].reshape(BLK, HD)[low : low + half_block]
        before = part(q_t[...], k, v, causal, before)
        top[...], acc[...] = before
        before = top[...], acc[...]

    pltpu.make_async_copy(pieces, pieces, spread_recv).wait()

    kv, half = kept(me)

    def pick(d):
        picked[d, 0] = pieces[sel[1, 0, d]]
        picked[d, 1] = pieces[sel[2, 0, d]]

    per_group = NZ // GROUPS
    pick(me)
    for _, d in others[:AHEAD]:
        pick(d)
    for t, (n, d) in enumerate(others):
        pltpu.make_async_remote_copy(
            src_ref=picked.at[d], dst_ref=fetched.at[n, kv, half], send_sem=fetch_send,
            recv_sem=fetch_recv.at[n // per_group], device_id={"ctx": d}, device_id_type=MESH,
        ).start()
        if t + AHEAD < NB - 1:
            pick(others[t + AHEAD][1])
    last = NZ - 1

    pltpu.make_async_copy(picked.at[me], fetched.at[last, kv, half], fetch_recv.at[GROUPS - 1]).start()
    gone = [jnp.where(sel[s + 1, 0, me] != me, 0.0, -jnp.inf).astype(jnp.float32) for s in range(2)]
    shape = (NB // NY // GROUPS * 4, PIECE, 1)
    slot = lax.broadcasted_iota(jnp.int32, shape, 0) % 2
    bias = jnp.where(slot == 0, gone[0], gone[1]).reshape(shape[0] * PIECE, 1)
    for g in range(GROUPS):
        planes = slice(g * (NZ // GROUPS), (g + 1) * (NZ // GROUPS))
        pltpu.make_async_copy(fetched.at[planes], fetched.at[planes], fetch_recv.at[g]).wait()
        k = fetched[planes, 0].reshape(-1, HD)
        v = fetched[planes, 1].reshape(-1, HD)
        before = part(q_t[...], k, v, lambda s: s + bias, (top[...], acc[...]))
        if g < GROUPS - 1:
            top[...], acc[...] = before
    total = before[1]
    share = 1.0 / total[HD : HD + 1]
    for h in range(QH):
        t = slice(h * BLK, (h + 1) * BLK)
        columns = slice(h * HD, (h + 1) * HD)
        out[:, columns] = (total[:HD, t] * share[:, t]).astype(out.dtype).T

    most = pl.ds(0, KVH - 1)
    pltpu.make_async_copy(own.at[:, most], own.at[:, most], head_send).wait()
    most = pl.ds(0, NB - 1)
    pltpu.make_async_copy(pieces.at[most], pieces.at[most], spread_send).wait()
    pltpu.make_async_copy(picked.at[most], picked.at[most], fetch_send).wait()


def on_device(queries, keys, values, selected):
    dma = pltpu.SemaphoreType.DMA
    hbm = pl.BlockSpec(memory_space=pl.ANY)
    return pl.pallas_call(
        kernel,
        out_shape=pltpu.VMEM((BLK, QH * HD), jnp.bfloat16),
        in_specs=[hbm, hbm, hbm, hbm],
        out_specs=pl.BlockSpec(memory_space=pltpu.VMEM),
        scratch_shapes=[
            pltpu.VMEM((BLK, QH * HD), jnp.bfloat16),
            pltpu.VMEM((HD, QH * BLK), jnp.bfloat16),
            pltpu.SMEM((3, 1, NB), jnp.int32),
            pltpu.VMEM((2, KVH, SLICE, HD), jnp.bfloat16),
            pltpu.VMEM((NB, PIECE, HD), jnp.bfloat16),
            pltpu.VMEM((NB, 2, PIECE, HD), jnp.bfloat16),
            pltpu.VMEM((NZ, 2, 2, 2, PIECE, HD), jnp.bfloat16),
            pltpu.VMEM((1, QH * BLK), jnp.float32),
            pltpu.VMEM((HD + PIECE, QH * BLK), jnp.float32),
            dma, dma, dma, dma((KVH,)), dma, dma, dma, dma((GROUPS,)),
        ],
        compiler_params=pltpu.CompilerParams(collective_id=0, has_side_effects=True),
    )(queries, keys, values, selected.transpose(2, 0, 1))


def solution(mesh):
    return jax.shard_map(
        on_device,
        mesh=mesh,
        in_specs=(
            P("ctx", "head"),
            P(("ctx", "head"), None),
            P(("ctx", "head"), None),
            P("head", None, None),
        ),
        out_specs=P("ctx", "head"),
        check_vma=False,
    )
```
